32 devices in a mesh: region: 4 (over x, core), subj: 8 (over z, y).
Axes of the slice: x: 2, y: 2, z: 4, core: 2. Of those that a mesh axis runs over, the one named last changes fastest.
Arguments:
- coords: float32 [2048, 3, 2048], P('subj', None, 'region'), may hold values from -30 to 30
- transform: float32 [2048, 3, 3], P('subj'), may hold values from -3.5 to 3.5
- labels: int32 [2048, 1], P('region'), may hold values from 0 to 3; in each aligned block of 512 rows (0 to 511, 512 to 1023, ...) at most 256 rows name the same one
- subject_order: int32 [2048], replicated, may hold values from 0 to 2047, each once
Outputs:
- region_gram: float32 [4, 2048, 2048], P('region', 'subj')
The draws below stay inside these ranges and needn't reach their ends.
Inputs may be any that keep to these rules, and one draw needn't show every extreme that they name: `labels`: among the 512 vertices of one device no region label occurs more than 256 times, and some label reaches 256. `subject_order`: a permutation of the subjects.
All inputs are finite; a program needn't handle non-finite values.
Results may differ from the reference program's by a relative error of at most 0.0012.
Values may be sent and summed in bfloat16 or wider, within the bound.
No kernel may reach another device: no remote copies, remote signals or barrier semaphores. Data moves between devices by JAX's collectives and lax.ppermute only.
A program may use at most 128 MiB of HBM per device.

```python
import math
import jax
import jax.numpy as jnp
import numpy as np
from jax import lax

SUBJECTS = 2048
V_DEV = 512
CAP = 256
VERTS = 2048
REGIONS = 4


def draw_coords(key, part):
    key_offset, key_shift, key_noise = jax.random.split(key, 3)
    position = jnp.arange(VERTS, dtype=jnp.float32) / VERTS
    offset = jax.random.uniform(key_offset, (1, 3, 1), jnp.float32, 1.0, 2.5)
    shift = 1.5 * jax.random.normal(key_shift, (SUBJECTS, 3, 1), jnp.float32)
    noise = 2.5 * jax.random.normal(key_noise, (SUBJECTS, 3, VERTS), jnp.float32)
    values = offset * (1.0 + 2.0 * position)[None, None, :] + shift + noise
    return jnp.clip(values, -30.0, 30.0).astype(jnp.float32)


def steps_of(rng, shape, shards, smallest, largest):
    factor_of = 1.0
    for dim, shards_of in shards:
        steps = jax.random.uniform(jax.random.fold_in(jax.random.fold_in(rng, 6), dim), (shards_of,), jnp.float32, smallest / len(shards), largest / len(shards))
        factor_of = factor_of * jnp.repeat(jnp.exp(steps), shape[dim] // shards_of).reshape((-1,) + (1,) * (len(shape) - 1 - dim))
    return factor_of


def assign_block(stream_key, own, number, rows, amount, top, reach, lean):
    ranking = jax.random.permutation(stream_key, amount)
    packed, common = portions_of(amount, rows * top, reach, lean, True), portions_of(amount, rows * top, reach, lean, False)
    places = jnp.arange(amount)

    def named(lengths, turn):
        used = int((lengths > 0).sum())
        fixed = max(1, used // 4)
        moved = fixed + (places - fixed + turn * (used - fixed)) % max(1, amount - fixed)
        return jnp.zeros((amount,), jnp.int32).at[ranking[jnp.where(places < fixed, places, moved)]].set(jnp.asarray(lengths, jnp.int32))

    lengths = jnp.where(number % 4 == 0, named(packed, number // 4), named(common, number - number // 4 - 1))
    mixed = jax.random.permutation(jax.random.fold_in(own, 3), amount)
    donor, receiver = mixed[0:amount // 2 * 2:2], mixed[1:amount // 2 * 2:2]
    slack = jnp.minimum(lengths[donor] - 1, reach - lengths[receiver]) // 2
    slack = jnp.where((donor == ranking[0]) | (receiver == ranking[0]) | (lengths[receiver] == 0), 0, jnp.maximum(slack, 0))
    moved = jax.random.randint(jax.random.fold_in(own, 4), (amount // 2,), 0, 1 << 20) % (slack + 1)
    lengths = lengths.at[donor].add(-moved).at[receiver].add(moved)
    items = jnp.searchsorted(jnp.cumsum(lengths), jnp.arange(rows * top), side="right").astype(jnp.int32)
    listing = items.reshape(top, rows).T
    listing = listing[jax.random.permutation(jax.random.fold_in(own, 1), rows)]
    turn = jax.random.randint(jax.random.fold_in(own, 2), (rows, 1), 0, top)
    return jnp.take_along_axis(listing, (jnp.arange(top)[None, :] + turn) % top, axis=1)


def portions_of(number_of, total, reach, skew, full):
    weights = [(1 << 20) // math.isqrt(grade ** skew) + 1 for grade in range(1, number_of + 1)]
    largest = reach if full else min(reach, max(-(-total // number_of), total * weights[0] // sum(weights)))
    least = 1 if total - largest >= number_of - 1 else 0
    counts, surplus = [largest] + [least] * (number_of - 1), total - largest - least * (number_of - 1)
    while surplus > 0:
        movable = [i for i in range(1, number_of) if counts[i] < largest] or [i for i in range(1, number_of) if counts[i] < reach]
        mass, left = sum([weights[i] for i in movable]), surplus
        for i in movable:
            more = min(reach - counts[i], max(1, left * weights[i] // mass), surplus)
            counts[i] = counts[i] + more
            surplus = surplus - more
    return np.array(counts)


def gaussian(stream_key, shape, width, limit, cuts=(), kind=jnp.bfloat16):
    drawn = width * jax.random.normal(stream_key, shape, jnp.float32)
    if cuts:
        drawn = drawn * steps_of(stream_key, shape, cuts, -0.22, 0.18)
    return jnp.clip(drawn, -limit, limit).astype(kind)


def setup_inputs(seed: int = 0) -> dict:
    seeds = jax.random.split(jax.random.key(seed), 5)
    coords = draw_coords(jax.random.fold_in(seeds[4], 71), 0)
    transform = gaussian(seeds[1], (SUBJECTS, 3, 3), 3 ** -0.5, 3.5, ((0, 8),), jnp.float32)
    labels_keys = jax.random.split(jax.random.fold_in(seeds[2], 1), VERTS // V_DEV)
    labels_turns = jax.random.permutation(jax.random.fold_in(seeds[2], 3), VERTS // V_DEV)
    labels = jax.vmap(lambda own, number: assign_block(jax.random.fold_in(seeds[2], 2), own, number, V_DEV, REGIONS, 1, CAP, 2))(labels_keys, labels_turns).reshape((VERTS, 1))
    subject_order = jax.random.permutation(seeds[3], SUBJECTS).astype(jnp.int32)
    return dict(coords=coords, transform=transform, labels=labels, subject_order=subject_order)


def reference(coords, transform, labels, subject_order):
    moved = (transform[:, :, 0:1] * coords[:, 0:1, :]
             + transform[:, :, 1:2] * coords[:, 1:2, :]
             + transform[:, :, 2:3] * coords[:, 2:3, :])
    centroid = jnp.sum(moved, axis=2, keepdims=True) / VERTS
    centered = (moved - centroid).astype(jnp.bfloat16)
    flat = centered.reshape(SUBJECTS, 3 * VERTS)
    label_row = labels[:, 0]
    scale = 1.0 / (3.0 * VERTS)

    def one_region(region_id):
        keep = (label_row == region_id)[None, None, :]
        masked = jnp.where(keep, centered, jnp.zeros_like(centered)).reshape(SUBJECTS, 3 * VERTS)
        gram = lax.dot_general(masked, flat, (((1,), (1,)), ((), ())), preferred_element_type=jnp.float32)
        gram = gram * scale
        return jnp.take(gram, subject_order, axis=1)

    return lax.map(one_region, jnp.arange(REGIONS, dtype=jnp.int32))
```

```python
import functools

import jax
import jax.numpy as jnp
from jax import lax
from jax.experimental import pallas as pl
from jax.experimental.pallas import tpu as pltpu
from jax.sharding import PartitionSpec as P

F32, BF16 = jnp.float32, jnp.bfloat16
NT = (((1,), (1,)), ((), ()))
NN = (((1,), (0,)), ((), ()))


def call(body, outs, name, cost=(0, 0), aliases=None):
    return pl.pallas_call(
        body,
        out_shape=outs,
        name=name,
        input_output_aliases=aliases or {},
        cost_estimate=pl.CostEstimate(flops=cost[0], bytes_accessed=cost[1], transcendentals=0),
    )


def sum_body(c_ref, o_ref):
    per = c_ref.shape[1]
    lane = lax.broadcasted_iota(jnp.int32, (per, 128), 1)
    cols = [jnp.sum(c_ref[d], axis=1, keepdims=True) for d in range(3)]
    wide = jnp.where(lane == 0, cols[0], jnp.where(lane == 1, cols[1], cols[2]))
    o_ref[...] = wide.T[:8]


def center_body(verts, regions, c_ref, t_ref, lab_ref, lab1_ref, *rest):
    sums, (o_ref, w_ref) = rest[:regions], rest[regions:]
    per, nv = c_ref.shape[1], c_ref.shape[2]
    total = sums[0][...]
    for s in sums[1:]:
        total = total + s[...]
    row = lax.broadcasted_iota(jnp.int32, (128, per), 0)
    flat = jnp.zeros((128, per), F32)
    for c in range(3):
        cen = jnp.zeros((1, per), F32)
        for d in range(3):
            t = t_ref[c, d : d + 1, :]
            flat = jnp.where(row == 3 * c + d, t, flat)
            cen = cen + t * total[d : d + 1]
        flat = jnp.where(row == 9 + c, cen / verts, flat)
    cols = flat.T
    step = 64
    for lo in range(0, per, step):
        x = [c_ref[d, lo : lo + step, :] for d in range(3)]
        for c in range(3):
            k = [cols[lo : lo + step, 3 * c + d : 3 * c + d + 1] for d in range(3)]
            cen = cols[lo : lo + step, 9 + c : 10 + c]
            moved = k[0] * x[0] + k[1] * x[1] + k[2] * x[2]
            o_ref[lo : lo + step, c * nv : (c + 1) * nv] = (moved - cen).astype(BF16)
    me = lax.axis_index("region")
    wrow = lax.broadcasted_iota(jnp.int32, (16, nv), 0)
    want = jnp.where(wrow % 2 == 0, me, me ^ 2)
    have = jnp.where(wrow < 2, lab_ref[...], lab1_ref[...])
    w = jnp.where(want == have, 1.0, 0.0).astype(BF16)
    for c in range(3):
        w_ref[:, c * nv : (c + 1) * nv] = w


def unit_body(units, panels, w_ref, *refs):
    ins, (keep_ref, send_ref) = refs[: 2 * panels], refs[2 * panels :]
    col = 0
    for left, right, lo, hi in units:
        a0, a1 = ins[2 * left][...], ins[2 * left + 1][...]
        b0, b1 = ins[2 * right][lo:hi, :], ins[2 * right + 1][lo:hi, :]
        for k, out in ((0, keep_ref), (1, send_ref)):
            g = lax.dot_general(a0 * w_ref[k : k + 1, :], b0, NT, preferred_element_type=F32)
            g += lax.dot_general(a1 * w_ref[k + 2 : k + 3, :], b1, NT, preferred_element_type=F32)
            out[:, col : col + hi - lo] = g
        col += hi - lo


def run_units(w, panels, units, name):
    per, depth = panels[0][0].shape
    width = sum(u[3] - u[2] for u in units)
    shape = jax.ShapeDtypeStruct((per, width), F32)
    flat = [x for pair in panels for x in pair]
    cost = (8 * per * width * depth, 2 * len(flat) * per * depth + 8 * per * width)
    body = functools.partial(unit_body, units, len(panels))
    return call(body, (shape, shape), name, cost)(w, *flat)


def place_body(blocks, n, scale, first, last, order_ref, *refs):
    o_ref = refs[-1]
    ins = refs[:-1]
    if not first:
        acc_ref, ins = ins[0], ins[1:]
    per = o_ref.shape[-2]
    total = o_ref.shape[-1]
    s = lax.axis_index("subj")
    pos = jnp.where(s % 2 == 0, s // 2, n - 1 - s // 2)
    vals, bases = [], []
    i = 0
    for d, parts, lo, hi in blocks:
        v = ins[i][...]
        for j in range(1, parts):
            v = v + ins[i + j][...]
        i += parts
        v = v * scale
        h = v.astype(BF16)
        vals.append((h, (v - h.astype(F32)).astype(BF16)))
        q = (pos + d + n) % n
        bases.append(jnp.where(q < n // 2, 2 * q, 2 * (n - 1 - q) + 1) * per + lo)
    step = 512
    for c in range(0, total, step):
        want = order_ref[:, c : c + step]
        acc = None if first else acc_ref[:, c : c + step]
        for (h, l), base, (_, _, lo, hi) in zip(vals, bases, blocks):
            row = lax.broadcasted_iota(jnp.int32, (hi - lo, step), 0) + base
            hot = jnp.where(row == want, 1.0, 0.0).astype(BF16)
            g = lax.dot_general(h, hot, NN, preferred_element_type=F32)
            g += lax.dot_general(l, hot, NN, preferred_element_type=F32)
            acc = g if acc is None else acc + g
        if last:
            o_ref[0, :, c : c + step] = acc
        else:
            o_ref[:, c : c + step] = acc


def place(order, acc, blocks, n, scale, last, name):
    per = blocks[0][1][0].shape[0]
    total = order.shape[1]
    meta = tuple((d, len(v), lo, hi) for d, v, lo, hi in blocks)
    flat = [x for _, v, _, _ in blocks for x in v]
    body = functools.partial(place_body, meta, n, scale, acc is None, last)
    shape = (1, per, total) if last else (per, total)
    width = sum(b[3] - b[2] for b in blocks)
    cost = (4 * per * width * total, 8 * per * total)
    args = (order,) + (() if acc is None else (acc,)) + tuple(flat)
    return call(body, jax.ShapeDtypeStruct(shape, F32), name, cost)(*args)


def local(n, regions, coords, transform, labels, order):
    per, nv = coords.shape[0], coords.shape[2]
    verts = nv * regions
    scale = 1.0 / (3.0 * verts)
    reach = n // 4
    half = per // 2
    ring = list(range(0, n, 2)) + list(range(n - 1, 0, -2))

    def hop(x, d):
        return lax.ppermute(x, "subj", [(ring[i], ring[(i + d) % n]) for i in range(n)])

    def swap(x, bit):
        return lax.ppermute(x, "region", [(r, r ^ bit) for r in range(regions)])

    c3 = jnp.transpose(coords, (1, 0, 2))
    t3 = jnp.transpose(transform, (1, 2, 0))
    lab = labels.reshape(1, nv)
    order = order.reshape(1, -1)
    sums = call(sum_body, jax.ShapeDtypeStruct((8, per), F32), "sums")(c3)
    lab1 = swap(lab, 1)
    others = [swap(sums, k) for k in range(1, regions)]
    own, w = call(
        functools.partial(center_body, verts, regions),
        (jax.ShapeDtypeStruct((per, 3 * nv), BF16), jax.ShapeDtypeStruct((16, 3 * nv), BF16)),
        "center",
    )(c3, t3, lab, lab1, sums, *others)

    panel = {0: own}
    for t in range(1, reach + 1):
        panel[-t] = hop(panel[-(t - 1)], 1)
        panel[t] = hop(panel[t - 1], -1)
    both = {d: (x, swap(x, 1)) for d, x in panel.items()}

    acc = None
    keep, send = run_units(w, [both[0]], ((0, 0, 0, per),), "unit0")
    ready = [(0, [keep, swap(send, 2)], 0, per)]
    for t in range(1, reach):
        for d in (-t, t):
            keep, send = run_units(w, [both[0], both[d]], ((0, 1, 0, per),), f"unit{d}")
            ready.append((d, [keep, swap(send, 2)], 0, per))
    acc = place(order, None, ready, n, scale, False, "place0")

    ready = []
    far = []
    for sign in (1, -1):
        d = sign * reach
        lo, hi = (0, half) if sign > 0 else (half, per)
        keep, send = run_units(w, [both[-d], both[d]], ((0, 1, lo, hi),), f"far{d}")
        far.append((d, keep + swap(send, 2), lo, hi))
    for sign in (1, -1):
        d = sign * reach
        for e in range(1, reach):
            keep, send = run_units(w, [both[-sign * e], both[d]], ((0, 1, 0, per),), f"mid{d}_{e}")
            got = hop(keep + swap(send, 2), -sign * e)
            ready.append((sign * (reach + e), [got], 0, per))
    for d, x, lo, hi in far:
        ready.append((2 * d, [hop(x, -d)], lo, hi))
    for d in (-reach, reach):
        keep, send = run_units(w, [both[0], both[d]], ((0, 1, 0, per),), f"unit{d}")
        ready.append((d, [keep, swap(send, 2)], 0, per))
    return place(order, acc, ready, n, scale, True, "place1")


def solution(mesh):
    placed = (P("subj", None, "region"), P("subj", None, None), P("region", None), P())
    body = functools.partial(local, mesh.shape["subj"], mesh.shape["region"])
    return jax.shard_map(
        body, mesh=mesh, in_specs=placed, out_specs=P("region", "subj", None), check_vma=False
    )
```

```python
import functools

import jax
import jax.numpy as jnp
from jax import lax
from jax.experimental import pallas as pl
from jax.experimental.pallas import tpu as pltpu
from jax.sharding import PartitionSpec as P

F32, BF16, I16 = jnp.float32, jnp.bfloat16, jnp.int16
NT = (((1,), (1,)), ((), ()))
NN = (((1,), (0,)), ((), ()))
VMEM = pl.BlockSpec(memory_space=pltpu.VMEM)
PAD = 16


def call(body, outs, name, args, cost=(0, 0), scratch=()):
    return pl.pallas_call(
        body,
        out_shape=outs,
        in_specs=[VMEM] * len(args),
        out_specs=jax.tree.map(lambda _: VMEM, outs),
        scratch_shapes=list(scratch),
        name=name,
        cost_estimate=pl.CostEstimate(flops=cost[0], bytes_accessed=cost[1], transcendentals=0),
    )(*args)


def shaped(*shape, dtype=F32):
    return jax.ShapeDtypeStruct(shape, dtype)


def encode(g, ref):
    rows = g.shape[0]
    top = jnp.max(jnp.abs(g), axis=0, keepdims=True)
    e = jnp.ceil(jnp.log(jnp.maximum(top, 1e-30)) * 1.4426950408889634 - 14.965784284662087)
    ref[:rows, :] = jnp.round(g * jnp.exp2(-e)).astype(jnp.int32).astype(I16)
    ref[rows:, :] = jnp.broadcast_to(e, (PAD, g.shape[1])).astype(jnp.int32).astype(I16)


def decode(ref):
    rows = ref.shape[0] - PAD
    e = ref[rows:, :].astype(jnp.int32).astype(F32)[:1]
    return ref[:rows, :].astype(jnp.int32).astype(F32) * jnp.exp2(e)


def sum_body(c_ref, o_ref):
    per = c_ref.shape[1]
    lane = lax.broadcasted_iota(jnp.int32, (per, 128), 1)
    cols = [jnp.sum(c_ref[d], axis=1, keepdims=True) for d in range(3)]
    wide = jnp.where(lane == 0, cols[0], jnp.where(lane == 1, cols[1], cols[2]))
    o_ref[...] = wide.T[:8]


def center_body(verts, regions, half, c_ref, t_ref, *rest):
    sums, o_ref = rest[:regions], rest[regions]
    per, nv = c_ref.shape[1], c_ref.shape[2]
    total = sums[0][...]
    for s in sums[1:]:
        total = total + s[...]
    row = lax.broadcasted_iota(jnp.int32, (128, per), 0)
    flat = jnp.zeros((128, per), F32)
    for c in range(3):
        cen = jnp.zeros((1, per), F32)
        for d in range(3):
            t = t_ref[c, d : d + 1, :]
            flat = jnp.where(row == 3 * c + d, t, flat)
            cen = cen + t * total[d : d + 1]
        flat = jnp.where(row == 9 + c, cen / verts, flat)
    rows = per // 2
    cols = flat[:, half * rows : (half + 1) * rows].T
    step = 64
    for lo in range(0, rows, step):
        at = half * rows + lo
        x = [c_ref[d, at : at + step, :] for d in range(3)]
        for c in range(3):
            k = [cols[lo : lo + step, 3 * c + d : 3 * c + d + 1] for d in range(3)]
            cen = cols[lo : lo + step, 9 + c : 10 + c]
            moved = k[0] * x[0] + k[1] * x[1] + k[2] * x[2]
            o_ref[lo : lo + step, c * nv : (c + 1) * nv] = (moved - cen).astype(BF16)


def mask_body(lab_ref, lab1_ref, w_ref):
    nv = lab_ref.shape[1]
    me = lax.axis_index("region")
    row = lax.broadcasted_iota(jnp.int32, (16, nv), 0)
    want = jnp.where(row % 2 == 0, me, me ^ 2)
    have = jnp.where(row < 2, lab_ref[...], lab1_ref[...])
    w = jnp.where(want == have, 1.0, 0.0).astype(BF16)
    for c in range(3):
        w_ref[:, c * nv : (c + 1) * nv] = w


def unit_body(lefts, rights, coded, w_ref, *refs):
    ins, (keep_ref, send_ref, l_ref, r_ref) = refs[:-4], refs[-4:]
    half, depth = ins[0].shape
    m = half * len(lefts)
    for core in range(2):
        at = slice(core * depth, (core + 1) * depth)
        for i, x in enumerate(lefts):
            for k in range(2):
                mask = w_ref[2 * core + k : 2 * core + k + 1, :]
                l_ref[k * m + i * half : k * m + (i + 1) * half, at] = ins[2 * x + core][...] * mask
        for i, x in enumerate(rights):
            r_ref[i * half : (i + 1) * half, at] = ins[2 * x + core][...]
    g = lax.dot_general(l_ref[...], r_ref[...], NT, preferred_element_type=F32)
    keep_ref[...] = g[:m]
    if coded:
        encode(g[m:], send_ref)
    else:
        send_ref[...] = g[m:]


def unit(w, lefts, rights, name, coded=True):
    halves = []
    place_of = {}
    for x in lefts + rights:
        if id(x) not in place_of:
            place_of[id(x)] = len(halves)
            halves.append(x)
    half, depth = halves[0][0].shape
    m, n = half * len(lefts), half * len(rights)
    body = functools.partial(
        unit_body, [place_of[id(x)] for x in lefts], [place_of[id(x)] for x in rights], coded
    )
    outs = (shaped(m, n), shaped(m + PAD, n, dtype=I16) if coded else shaped(m, n))
    args = (w, *[y for x in halves for y in x])
    scratch = [pltpu.VMEM((2 * m, 2 * depth), BF16), pltpu.VMEM((n, 2 * depth), BF16)]
    return call(body, outs, name, args, (8 * m * n * depth, 4 * len(halves) * half * depth), scratch)


def merge_body(keep_ref, got_ref, o_ref):
    encode(keep_ref[...] + decode(got_ref), o_ref)


def merge(keep, got, name):
    return call(merge_body, shaped(*got.shape, dtype=I16), name, (keep, got), (0, 8 * keep.size))


def value(refs):
    parts = [decode(r) if r.dtype == I16 else r[...] for r in refs]
    return parts[0] if len(parts) == 1 else parts[0] + parts[1]


def place_body(blocks, n, scale, first, last, order_ref, *refs):
    o_ref, ins = refs[-1], refs[:-1]
    if not first:
        acc_ref, ins = ins[0], ins[1:]
    per, total = o_ref.shape[-2], o_ref.shape[-1]
    s = lax.axis_index("subj")
    pos = jnp.where(s % 2 == 0, s // 2, n - 1 - s // 2)
    vals, bases = [], []
    i = 0
    for d, strips, lo, hi in blocks:
        rows = []
        for count in strips:
            rows.append(value(ins[i : i + count]))
            i += count
        v = (rows[0] if len(rows) == 1 else jnp.concatenate(rows, axis=0)) * scale
        h = v.astype(BF16)
        vals.append(jnp.concatenate([h, (v - h.astype(F32)).astype(BF16)], axis=0))
        q = (pos + d + n) % n
        bases.append(jnp.where(q < n // 2, 2 * q, 2 * (n - 1 - q) + 1) * per + lo)
    step = 512
    for c in range(0, total, step):
        want = order_ref[:, c : c + step]
        acc = None if first else acc_ref[:, c : c + step]
        for hl, base, (_, _, lo, hi) in zip(vals, bases, blocks):
            row = lax.broadcasted_iota(jnp.int32, (hi - lo, step), 0) + base
            hot = jnp.where(row == want, 1.0, 0.0).astype(BF16)
            g = lax.dot_general(hl, hot, NN, preferred_element_type=F32)
            g = g[:per] + g[per:]
            acc = g if acc is None else acc + g
        if last:
            o_ref[0, :, c : c + step] = acc
        else:
            o_ref[:, c : c + step] = acc


def place(order, acc, blocks, n, per, scale, last, name):
    total = order.shape[1]
    meta = tuple((d, tuple(len(p) for p in strips), lo, hi) for d, strips, lo, hi in blocks)
    flat = [x for _, strips, _, _ in blocks for p in strips for x in p]
    body = functools.partial(place_body, meta, n, scale, acc is None, last)
    shape = (1, per, total) if last else (per, total)
    width = sum(b[3] - b[2] for b in blocks)
    args = (order,) + (() if acc is None else (acc,)) + tuple(flat)
    return call(body, shaped(*shape), name, args, (4 * per * width * total, 8 * per * total))


def gate(x, *after):
    return lax.optimization_barrier((x, *after))[0]


def local(n, regions, coords, transform, labels, order):
    per, nv = coords.shape[0], coords.shape[2]
    verts = nv * regions
    scale = 1.0 / (3.0 * verts)
    reach = n // 4
    half = per // 2
    ring = list(range(0, n, 2)) + list(range(n - 1, 0, -2))

    def hop(x, d):
        return lax.ppermute(x, "subj", [(ring[i], ring[(i + d) % n]) for i in range(n)])

    def swap(x, bit):
        return lax.ppermute(x, "region", [(r, r ^ bit) for r in range(regions)])

    c3 = jnp.transpose(coords, (1, 0, 2))
    t3 = jnp.transpose(transform, (1, 2, 0))
    lab = labels.reshape(1, nv)
    order = order.reshape(1, -1)
    sums = call(sum_body, shaped(8, per), "sums", (c3,))
    others = [swap(sums, k) for k in range(1, regions)]
    lab1 = swap(lab, 1)
    own = []
    for h in range(2):
        body = functools.partial(center_body, verts, regions, h)
        args = (c3, t3, sums, *others)
        own.append(call(body, shaped(half, 3 * nv, dtype=BF16), f"center{h}", args))
    w = call(mask_body, shaped(16, 3 * nv, dtype=BF16), "masks", (lab, lab1))

    panel = {0: [(x, swap(x, 1)) for x in own]}
    keep, send = unit(w, panel[0], panel[0], "unit0", coded=False)
    ready = [(0, [[keep, swap(send, 2)]], 0, per)]
    after = keep
    raw = {0: own}
    strips = {}
    for t in range(1, reach + 1):
        for d in (-t, t):
            raw[d] = [None, None]
        for h in range(2):
            for d in (-t, t):
                s = 1 if d < 0 else -1
                x = raw[d + s][h]
                raw[d][h] = hop(x if t == 1 else gate(x, after), s)
        for d in (-t, t):
            panel[d] = [None, None]
        if t < reach:
            for h in range(2):
                for d in (-t, t):
                    panel[d][h] = (raw[d][h], swap(raw[d][h], 1))
            for d in (-t, t):
                keep, send = unit(w, panel[0], panel[d], f"unit{d}")
                ready.append((d, [[keep, swap(send, 2)]], 0, per))
                after = keep
    acc = place(order, None, ready, n, per, scale, False, "place0")

    r = reach
    for d in (-r, r):
        x = gate(raw[d][0], after)
        panel[d][0] = (x, swap(x, 1))
    keep0, send0 = unit(w, panel[0], [panel[-r][0], panel[r][0]], "near0")
    got0 = swap(send0, 2)
    for d in (-r, r):
        x = gate(raw[d][1], keep0, acc)
        panel[d][1] = (x, swap(x, 1))
    out = {}
    for e in range(1, r):
        for s in (1, -1):
            keep, send = unit(w, panel[-s * e], panel[s * r], f"mid{s}_{e}")
            out[s, e] = (keep, swap(send, 2))
    for s in (1, -1):
        keep, send = unit(w, [panel[-s * r][0 if s > 0 else 1]], panel[s * r], f"far{s}")
        out[s, r] = (keep, swap(send, 2))
    keep1, send1 = unit(w, panel[0], [panel[-r][1], panel[r][1]], "near1")
    got1 = swap(send1, 2)
    res = {}
    for (s, e), (keep, got) in out.items():
        res[s, e] = hop(merge(keep, got, f"merge{s}_{e}"), -s * e)
    near = []
    for i, d in enumerate((-r, r)):
        for h, (keep, got) in enumerate(((keep0, got0), (keep1, got1))):
            at = slice(i * half, (i + 1) * half)
            near.append((d, [[keep[:, at], got[:, at]]], h * half, (h + 1) * half))
    acc = place(order, acc, near, n, per, scale, False, "place1")
    tail = [(s * (r + e), [[res[s, e]]], 0, per) for e in range(1, r) for s in (1, -1)]
    tail.append((2 * r, [[res[1, r]], [res[-1, r]]], 0, per))
    return place(order, acc, tail, n, per, scale, True, "place2")


def solution(mesh):
    placed = (P("subj", None, "region"), P("subj", None, None), P("region", None), P())
    body = functools.partial(local, mesh.shape["subj"], mesh.shape["region"])
    return jax.shard_map(
        body, mesh=mesh, in_specs=placed, out_specs=P("region", "subj", None), check_vma=False
    )
```
